512 devices in a mesh: tm: 128 (over z, y, core), mod: 4 (over x).
Axes of the slice: x: 4, y: 4, z: 16, core: 2. Of those that a mesh axis runs over, the one named last changes fastest.
Arguments:
- filterbank: bfloat16 [16384, 128], P('tm'), may hold values from -6 to 6
- conv_weight: bfloat16 [384, 1280], replicated, may hold values from -0.3125 to 0.3125
- mlp_gain: float32 [1280], replicated, may hold values from 0.25 to 1.75
- up_weight: bfloat16 [1280, 5120], P('tm', 'mod'), may hold values from -0.15625 to 0.15625
- down_weight: bfloat16 [5120, 1280], P('mod', 'tm'), may hold values from -0.078125 to 0.078125
- post_gain: float32 [1280], replicated, may hold values from 0.25 to 1.75
- audio_weight: bfloat16 [1280, 1792], P(None, 'mod'), may hold values from -0.15625 to 0.15625
- patches: bfloat16 [32768, 1280], P('tm'), may hold values from -6 to 6
- vision_gain: float32 [1280], replicated, may hold values from 0.25 to 1.75
- vision_weight: bfloat16 [5120, 1792], P('tm', 'mod'), may hold values from -0.078125 to 0.078125
- retention: int32 [128, 64], P('tm'), may hold values from 0 to 63, each once within a row
- kept_count: int32 [128], P('tm'), may hold values from 1 to 64, 4096 in all
Outputs:
- sequence: bfloat16 [128, 96, 1792], P('tm', None, 'mod')
The draws below stay inside these ranges and needn't reach their ends.
Inputs may be any that keep to these rules, and one draw needn't show every extreme that they name: `retention`: each row lists every merged token of its frame once. `kept_count`: the counts sum to 4096.
All inputs are finite; a program needn't handle non-finite values. No bound on the sum of `kept_count` on one device may be relied on, other than what follows from the above.
Results may differ from the reference program's by a relative error of at most 0.01.
Values may be sent and summed in bfloat16 or wider, within the bound.
No kernel may reach another device: no remote copies, remote signals or barrier semaphores. Data moves between devices by JAX's collectives and lax.ppermute only.
A program may use at most 64 MiB of HBM per device.

```python
import math
import jax
import jax.numpy as jnp
import numpy as np
from jax import lax

D_ENC = 1280
MEL = 128
D_HID = 5120
D_OUT = 1792
MRG_FRAME = 64
AUD_DEV = 128
AUD_TOK = 64
AUD_ALL = 16384
D_MRG = 5120
PATCH_ALL = 32768
KEEP_TOTAL = 4096
SEQ_DEV = 96
N_TM = 128


def level_of(stream_key, dims, pieces, low, high):
    loudness, own = 1.0, jax.random.fold_in(stream_key, 6)
    for axis_at, shards_of in pieces:
        heights = jnp.exp(jax.random.uniform(jax.random.fold_in(own, axis_at), (shards_of,), jnp.float32, low / len(pieces), high / len(pieces)))
        loudness = loudness * jnp.repeat(heights, dims[axis_at] // shards_of).reshape([-1 if axis == axis_at else 1 for axis in range(len(dims))])
    return loudness


def length_profile(amount, total, most, skew):
    loads = [(1 << 20) // math.isqrt(rank ** skew) + 1 for rank in range(2, amount + 1)]
    spare, counts = total - most - (amount - 1), [1] * (amount - 1)
    while spare > 0:
        free = [i for i in range(amount - 1) if counts[i] < most]
        whole, left = sum([loads[i] for i in free]), spare
        for i in free:
            extra = min(most - counts[i], max(1, left * loads[i] // whole), spare)
            counts[i] = counts[i] + extra
            spare = spare - extra
    return np.array([most] + counts)


def ragged(rng, number_of, total, reach, lean):
    if number_of == 2:
        one = jax.random.randint(rng, (), max(1, total - reach), min(reach, total - 1) + 1)
        return jnp.stack([one, total - one])
    lengths = jnp.asarray(length_profile(number_of, total, reach, lean), jnp.int32)
    twos = (number_of - 1) // 2
    giver, sink = lengths[1:1 + 2 * twos:2], lengths[2:2 + 2 * twos:2]
    slack = jnp.minimum(giver - 1, reach - sink)
    passed = jax.random.randint(jax.random.fold_in(rng, 1), (twos,), 0, 1 << 20) % (slack + 1)
    lengths = lengths.at[1:1 + 2 * twos:2].set(giver - passed).at[2:2 + 2 * twos:2].set(sink + passed)
    return lengths[jax.random.permutation(jax.random.fold_in(rng, 2), number_of)]


def gaussian(rng, extent, scale, most, shards=(), held_as=jnp.bfloat16):
    drawn = jax.random.normal(rng, extent, jnp.float32) * scale
    if len(shards) > 0:
        drawn = level_of(rng, extent, shards, -0.22, 0.18) * drawn
    return jnp.clip(drawn, min=-most, max=most).astype(held_as)


def setup_inputs(seed: int = 0) -> dict:
    seeds = jax.random.split(jax.random.key(seed), 13)
    filterbank = gaussian(seeds[0], (AUD_ALL, MEL), 1.0, 6.0, ((0, 128),))
    conv_weight = gaussian(seeds[1], (3 * MEL, D_ENC), (3 * MEL) ** -0.5, 0.3125)
    mlp_gain = jnp.clip(1.0 + 0.15 * jax.random.normal(seeds[2], (D_ENC,), jnp.float32), 0.25, 1.75)
    up_weight = gaussian(seeds[3], (D_ENC, D_HID), D_ENC ** -0.5, 0.15625, ((0, 128), (1, 4)))
    down_weight = gaussian(seeds[4], (D_HID, D_ENC), D_HID ** -0.5, 0.078125, ((0, 4), (1, 128)))
    post_gain = jnp.clip(1.0 + 0.15 * jax.random.normal(seeds[5], (D_ENC,), jnp.float32), 0.25, 1.75)
    audio_weight = gaussian(seeds[6], (D_ENC, D_OUT), D_ENC ** -0.5, 0.15625, ((1, 4),))
    patches = gaussian(seeds[7], (PATCH_ALL, D_ENC), 1.0, 6.0, ((0, 128),))
    vision_gain = jnp.clip(1.0 + 0.15 * jax.random.normal(seeds[8], (D_ENC,), jnp.float32), 0.25, 1.75)
    vision_weight = gaussian(seeds[9], (D_MRG, D_OUT), D_MRG ** -0.5, 0.078125, ((0, 128), (1, 4)))
    retention = jax.vmap(lambda own: jax.random.permutation(own, MRG_FRAME))(jax.random.split(seeds[10], N_TM)).reshape((N_TM, MRG_FRAME)).astype(jnp.int32)
    kept_count = ragged(seeds[11], N_TM, KEEP_TOTAL, MRG_FRAME, 2).astype(jnp.int32)
    return {"filterbank": filterbank, "conv_weight": conv_weight, "mlp_gain": mlp_gain, "up_weight": up_weight, "down_weight": down_weight, "post_gain": post_gain, "audio_weight": audio_weight, "patches": patches, "vision_gain": vision_gain, "vision_weight": vision_weight, "retention": retention, "kept_count": kept_count}


def layer_norm(values, scale_gain):
    average = lax.optimization_barrier(jnp.mean(values, axis=-1, keepdims=True))
    centred = values - average
    variance = lax.optimization_barrier(jnp.mean(centred * centred, axis=-1, keepdims=True))
    return centred * lax.rsqrt(variance + 1e-05) * scale_gain

def rms_norm(values, scale_gain):
    square_mean = lax.optimization_barrier(jnp.mean(values * values, axis=-1, keepdims=True))
    return values * lax.rsqrt(square_mean + 1e-06) * scale_gain

def encode_span(stem_rows, mlp_gain, up_weight, down_weight, post_gain, audio_weight):
    residual = stem_rows.astype(jnp.float32)
    hidden = layer_norm(residual, mlp_gain).astype(jnp.bfloat16)
    activated = jax.nn.gelu(jnp.dot(hidden, up_weight, preferred_element_type=jnp.float32), approximate=False).astype(jnp.bfloat16)
    mixed = residual + jnp.dot(activated, down_weight, preferred_element_type=jnp.float32)
    pooled = mixed.reshape(-1, 2, mixed.shape[-1]).mean(axis=1)
    normed = layer_norm(pooled, post_gain).astype(jnp.bfloat16)
    return jnp.dot(normed, audio_weight, preferred_element_type=jnp.float32).astype(jnp.bfloat16)

def reference(filterbank, conv_weight, mlp_gain, up_weight, down_weight, post_gain, audio_weight, patches, vision_gain, vision_weight, retention, kept_count):
    padded = jnp.pad(filterbank, ((1, 1), (0, 0)))
    unfolded = jnp.concatenate([padded[:-2], padded[1:-1], padded[2:]], axis=1)
    stem = jax.nn.gelu(jnp.dot(unfolded, conv_weight, preferred_element_type=jnp.float32), approximate=False).astype(jnp.bfloat16)
    spans = stem.reshape(N_TM, AUD_DEV, D_ENC)
    audio_tokens = lax.map(lambda rows: encode_span(rows, mlp_gain, up_weight, down_weight, post_gain, audio_weight), spans)
    audio_tokens = audio_tokens.reshape(N_TM * AUD_TOK, D_OUT)
    patch_normed = rms_norm(patches.astype(jnp.float32), vision_gain).astype(jnp.bfloat16)
    merged = patch_normed.reshape(N_TM * MRG_FRAME, D_MRG)
    visual_tokens = jnp.dot(merged, vision_weight, preferred_element_type=jnp.float32).astype(jnp.bfloat16)
    placed = (kept_count + AUD_TOK).astype(jnp.int32)
    starts = (jnp.cumsum(placed) - placed).astype(jnp.int32)
    total_len = SEQ_DEV * N_TM
    slot_range = jnp.arange(MRG_FRAME, dtype=jnp.int32)
    visual_pos = jnp.where(slot_range[None, :] < kept_count[:, None], starts[:, None] + slot_range[None, :], total_len).astype(jnp.int32)
    span_base = (jnp.arange(N_TM, dtype=jnp.int32) * MRG_FRAME)[:, None]
    visual_rows = jnp.take(visual_tokens, (span_base + retention).reshape(-1).astype(jnp.int32), axis=0)
    audio_pos = ((starts + kept_count)[:, None] + jnp.arange(AUD_TOK, dtype=jnp.int32)[None, :]).astype(jnp.int32)
    flat = jnp.zeros((total_len, D_OUT), jnp.bfloat16)
    flat = flat.at[visual_pos.reshape(-1)].set(visual_rows, mode='drop')
    flat = flat.at[audio_pos.reshape(-1)].set(audio_tokens, mode='drop')
    return flat.reshape(SEQ_DEV, N_TM, D_OUT).transpose(1, 0, 2)
```

```python
import jax
import jax.numpy as jnp
import numpy as np
from jax import lax
from jax.sharding import Mesh, PartitionSpec as P

MRG_FRAME = 64
AUD_TOK = 64
SEQ_DEV = 96
D_ENC = 1280
TM = ("z", "y", "c")
NZ, NY, NC, NM = 16, 4, 2, 4
N_TM = NZ * NY * NC
BF = jnp.bfloat16
F32 = jnp.float32


def feature_order():
    block = np.arange(N_TM)
    c, y, z = block // (NY * NZ), (block // NZ) % NY, block % NZ
    first = 10 * (8 * z + 2 * y + c)
    main = (first[:, None] + np.arange(8)[None, :]).reshape(-1)
    rest = (first[None, :] + 8 + np.arange(2)[:, None]).reshape(-1)
    return np.concatenate([main, rest]).astype(np.int32)


def gather(value, axis):
    peers = lax.axis_size(axis)
    spread = jnp.broadcast_to(value[None], (peers,) + value.shape)
    return lax.all_to_all(spread, axis, 0, 0)


def layer_norm(values, scale_gain):
    average = jnp.mean(values, axis=-1, keepdims=True)
    centred = values - average
    variance = jnp.mean(centred * centred, axis=-1, keepdims=True)
    return centred * lax.rsqrt(variance + 1e-05) * scale_gain


def rms_norm(values, scale_gain):
    square_mean = jnp.mean(values * values, axis=-1, keepdims=True)
    return values * lax.rsqrt(square_mean + 1e-06) * scale_gain


def halo(shard):
    up = [(i, i + 1) for i in range(N_TM - 1)]
    down = [(j, i) for i, j in up]
    before = lax.ppermute(shard[-1:], TM, up)
    after = lax.ppermute(shard[:1], TM, down)
    return jnp.concatenate([before, shard, after], axis=0)


def dot(a, b):
    return jnp.dot(a, b, preferred_element_type=F32)


def on_device(
    filterbank,
    conv_weight,
    mlp_gain,
    up_weight,
    down_weight,
    post_gain,
    audio_weight,
    patches,
    vision_gain,
    vision_weight,
    retention,
    kept_count,
):
    down_rows = down_weight.T
    rest = jnp.stack([up_weight[8:], down_rows[8:]])
    rest = rest.reshape(4, 2, 640).transpose(1, 0, 2).reshape(8, 640)
    ffn = jnp.concatenate([up_weight[:8], down_rows[:8], rest], axis=1)
    ffn = gather(ffn, "z")
    count_lane = jnp.broadcast_to(kept_count.astype(BF)[:, None], (40, 64))
    vis = jnp.concatenate([vision_weight, count_lane], axis=1)
    vis = gather(vis, "z")
    ffn = gather(ffn, "y")
    ffn = gather(ffn, "c").reshape(8 * N_TM, 3200)

    order = jnp.asarray(feature_order())
    pick = (lax.broadcasted_iota(jnp.int32, (D_ENC, D_ENC), 0) == order[None, :]).astype(BF)
    conv = dot(conv_weight, pick).astype(BF)
    audio_rows = lax.dot_general(
        pick, audio_weight, (((0,), (0,)), ((), ())), preferred_element_type=F32
    ).astype(BF)
    gains = jnp.dot(
        jnp.stack([mlp_gain, post_gain]), pick.astype(F32), precision=lax.Precision.HIGHEST
    )

    framed = halo(filterbank)
    unfolded = jnp.concatenate([framed[:-2], framed[1:-1], framed[2:]], axis=1)
    stem = jax.nn.gelu(dot(unfolded, conv), approximate=False).astype(BF)
    residual = stem.astype(F32)
    hidden = layer_norm(residual, gains[0]).astype(BF)
    pooled_stem = residual.reshape(64, 2, D_ENC).mean(axis=1)

    rest = ffn[:, 2560:].reshape(N_TM, 2, 4, 640).transpose(2, 0, 1, 3).reshape(4 * N_TM, 1280)
    pre_act = dot(hidden[:, :1024], ffn[:, :1280]) + dot(hidden[:, 1024:], rest[:256])
    activated = jax.nn.gelu(pre_act, approximate=False)
    activated = activated.reshape(64, 2, 1280).mean(axis=1).astype(BF)
    nt = (((1,), (1,)), ((), ()))
    partial_main = lax.dot_general(activated, ffn[:, 1280:2560], nt, preferred_element_type=F32)
    partial_rest = lax.dot_general(activated, rest[256:], nt, preferred_element_type=F32)
    part = jnp.concatenate([partial_main, partial_rest], axis=1)
    sent = part.astype(BF)
    total = part
    for shift in (1, 3, 2):
        moved = lax.ppermute(sent, "mod", [(i, (i + shift) % NM) for i in range(NM)])
        total = total + moved.astype(F32)
    normed = layer_norm(pooled_stem + total, gains[1]).astype(BF)
    audio_tokens = dot(normed, audio_rows).astype(BF)

    vis = gather(vis, "y")
    vis = gather(vis, "c")
    counts = vis[:, :, :, 0, 448].astype(jnp.int32).transpose(2, 1, 0).reshape(N_TM)
    patch_normed = rms_norm(patches.astype(F32), vision_gain).astype(BF)
    merged = patch_normed.reshape(MRG_FRAME, -1)
    vis_rows = vis.transpose(2, 1, 0, 3, 4).reshape(5120, 512)
    visual_tokens = dot(merged, vis_rows)[:, :448].astype(BF)

    me = lax.axis_index(TM).astype(jnp.int32)
    ids = jnp.arange(N_TM, dtype=jnp.int32)
    placed = counts + AUD_TOK
    starts = jnp.sum(jnp.where(ids[None, :] < ids[:, None], placed[None, :], 0), axis=1)
    kept = kept_count[0]
    first_slot = jnp.sum(jnp.where(ids < me, placed, 0))

    local = ((ids - first_slot) % N_TM)[:, None]
    ranks = jnp.arange(MRG_FRAME, dtype=jnp.int32)
    by_rank = (retention[0][:, None] == ranks[None, :]).astype(BF)
    ordered = dot(by_rank, visual_tokens).astype(BF)
    take_visual = ((local == ranks[None, :]) & (ranks[None, :] < kept)).astype(BF)
    take_audio = (local - kept == ranks[None, :]).astype(BF)
    send = dot(
        jnp.concatenate([take_visual, take_audio], axis=1),
        jnp.concatenate([ordered, audio_tokens], axis=0),
    ).astype(BF)
    moved = lax.all_to_all(send.reshape(NZ, NY * NC, 448), "z", 0, 0)
    moved = lax.all_to_all(moved.transpose(1, 0, 2), ("y", "c"), 0, 0)
    moved = moved.reshape(N_TM, 448)

    began = starts.reshape(NZ, NY * NC).T.reshape(N_TM)
    length = placed.reshape(NZ, NY * NC).T.reshape(N_TM)
    offset = (me - began) % N_TM
    slot = jnp.where(offset < length, (began + offset) // N_TM, -1)
    slots = jnp.arange(SEQ_DEV, dtype=jnp.int32)
    put = (slot[None, :] == slots[:, None]).astype(BF)
    return dot(put, moved).astype(BF)[None]


def solution(mesh):
    split = Mesh(mesh.devices.reshape(NZ, NY, NC, NM), TM + ("mod",))
    return jax.shard_map(
        on_device,
        mesh=split,
        in_specs=(
            P(TM, None),
            P(),
            P(),
            P(TM, "mod"),
            P("mod", TM),
            P(),
            P(None, "mod"),
            P(TM, None),
            P(),
            P(TM, "mod"),
            P(TM, None),
            P(TM),
        ),
        out_specs=P(TM, None, "mod"),
        check_vma=False,
    )
```

```python
import jax
import jax.numpy as jnp
from jax import lax
from jax.experimental import pallas as pl
from jax.experimental.pallas import tpu as pltpu
from jax.sharding import Mesh, PartitionSpec as P

MRG_FRAME = 64
AUD_TOK = 64
SEQ_DEV = 96
D_ENC = 1280
D_LM = 448
Z = ("zh", "zl")
TM = Z + ("y", "c")
NZ, NY, NC, NM = 16, 4, 2, 4
WIDE = 3328
N_TM = NZ * NY * NC

BF = jnp.bfloat16
F32 = jnp.float32
NT = (((1,), (1,)), ((), ()))
VMEM = pl.BlockSpec(memory_space=pltpu.VMEM)


def arrival_spans():
    zl, c = lax.axis_index("zl"), lax.axis_index("c")
    block = jnp.arange(N_TM, dtype=jnp.int32)
    hop, zh, z_hop = block // NZ, (block // 4) % 4, block % 4
    shift = lambda k: jnp.where(k == 2, 3, jnp.where(k == 3, 2, k))
    from_z = 4 * zh + (zl + 4 - shift(z_hop)) % 4
    from_y = hop % NY
    from_c = jnp.where(hop < NY, c, 1 - c)
    return (8 * from_z + 2 * from_y + from_c).astype(jnp.int32)


def around(value, axis, size):
    shifts = (1, size - 1, 2)
    return [value] + [
        lax.ppermute(value, axis, [(i, (i + shift) % size) for i in range(size)])
        for shift in shifts
    ]


def swap_core(value):
    return lax.ppermute(value, "c", [(0, 1), (1, 0)])


def layer_norm(values, scale_gain):
    average = jnp.mean(values, axis=-1, keepdims=True)
    centred = values - average
    variance = jnp.mean(centred * centred, axis=-1, keepdims=True)
    return centred * lax.rsqrt(variance + 1e-05) * scale_gain


def rms_norm(values, scale_gain):
    square_mean = jnp.mean(values * values, axis=-1, keepdims=True)
    return values * lax.rsqrt(square_mean + 1e-06) * scale_gain


def halo(shard):
    up = [(i, i + 1) for i in range(N_TM - 1)]
    down = [(j, i) for i, j in up]
    before = lax.ppermute(shard[-1:], TM, up)
    after = lax.ppermute(shard[:1], TM, down)
    return jnp.concatenate([before, shard, after], axis=0)


def dot(a, b):
    return jnp.dot(a, b, preferred_element_type=F32)


def erf_gelu(x):
    return 0.5 * x * (1.0 + lax.erf(x * 0.7071067811865476))


def pack_kernel(count_ref, up_ref, down_ref, vision_ref, out_ref):
    sides = (up_ref[8:].astype(F32), down_ref[8:].astype(F32))
    rest = [
        sides[row // 2][row % 2 : row % 2 + 1, 640 * half : 640 * half + 640]
        for half in range(2)
        for row in range(4)
    ]
    rest = jnp.concatenate(rest, axis=0).astype(BF)
    count = jnp.full((8, 128), count_ref[0].astype(F32), F32).astype(BF)
    blank = jnp.zeros((8, 64), BF)
    for peer in range(4):
        out_ref[peer, :, :1280] = up_ref[:8, :]
        out_ref[peer, :, 1280:2560] = down_ref[:8, :]
        out_ref[peer, :, 2560:3200] = rest
        out_ref[peer, :, 3200:WIDE] = count
        for k in range(5):
            start = WIDE + 512 * k
            rows = vision_ref[8 * k : 8 * k + 8, :]
            out_ref[peer, :, start : start + 512] = jnp.concatenate([rows, blank], axis=1)


def pack(kept_count, up_weight, down_rows, vision_weight):
    return pl.pallas_call(
        pack_kernel,
        out_shape=jax.ShapeDtypeStruct((4, 8, WIDE + 2560), BF),
        in_specs=[pl.BlockSpec(memory_space=pltpu.SMEM), VMEM, VMEM, VMEM],
        out_specs=VMEM,
        name="pack",
    )(kept_count, up_weight, down_rows, vision_weight)


def ffn_kernel(hidden_ref, own_ref, other_ref, out_ref, count_ref, up, down, flat):
    for c, ref in enumerate((own_ref, other_ref)):
        rows = slice(512 * c, 512 * c + 512)
        up[rows, :] = ref[:, :1280]
        down[rows, :] = ref[:, 1280:2560]
        for tile in range(6):
            lanes = slice(2560 + 128 * tile, 2688 + 128 * tile)
            flat[tile, rows, :] = ref[:, lanes].astype(F32)
    for tile in range(5):
        for half in range(2):
            lanes = slice(640 * half + 128 * tile, 640 * half + 128 * tile + 128)
            for row in range(4):
                plane = flat[tile, pl.ds(half * 4 + row, N_TM, stride=8), :].astype(BF)
                into = up if row < 2 else down
                start = 1024 + (row % 2) * N_TM
                into[start : start + N_TM, lanes] = plane
    count_ref[...] = flat[5, pl.ds(0, N_TM, stride=8), :]
    row = lax.broadcasted_iota(jnp.int32, (64, 128), 0)
    col = lax.broadcasted_iota(jnp.int32, (64, 128), 1)
    pair = jnp.where(col // 2 == row, 0.5, 0.0).astype(BF)
    act = erf_gelu(dot(hidden_ref[...], up[...])).astype(BF)
    pooled = dot(pair, act).astype(BF)
    part = lax.dot_general(pooled, down[...], NT, preferred_element_type=F32).astype(BF)
    for peer in range(NM):
        out_ref[peer] = part


def ffn(hidden, own, other):
    return pl.pallas_call(
        ffn_kernel,
        out_shape=(
            jax.ShapeDtypeStruct((NM, 64, D_ENC), BF),
            jax.ShapeDtypeStruct((N_TM, 128), F32),
        ),
        in_specs=[VMEM] * 3,
        out_specs=(VMEM, VMEM),
        scratch_shapes=[
            pltpu.VMEM((1280, 1280), BF),
            pltpu.VMEM((1280, 1280), BF),
            pltpu.VMEM((6, 1024, 128), F32),
        ],
        cost_estimate=pl.CostEstimate(
            flops=650_000_000, bytes_accessed=8_000_000, transcendentals=170_000
        ),
        name="ffn",
    )(hidden, own, other)


def tail_kernel(
    part_ref, stem_ref, gain_ref, audio_ref, mine_ref, theirs_ref, rank_ref, take_ref, out_ref
):
    total = stem_ref[...]
    for peer in range(NM):
        total = total + part_ref[peer].astype(F32)
    normed = layer_norm(total, gain_ref[...]).astype(BF)
    audio = dot(normed, audio_ref[...]).astype(BF)
    visual = (mine_ref[...] + theirs_ref[...].astype(F32)).astype(BF)
    visual = dot(rank_ref[...], visual).astype(BF)
    picked = dot(take_ref[:, :64], visual) + dot(take_ref[:, 64:], audio)
    out_ref[...] = picked.astype(BF)


def tail(*args):
    return pl.pallas_call(
        tail_kernel,
        out_shape=jax.ShapeDtypeStruct((N_TM, D_LM), BF),
        in_specs=[VMEM] * 8,
        out_specs=VMEM,
        cost_estimate=pl.CostEstimate(
            flops=80_000_000, bytes_accessed=2_500_000, transcendentals=64
        ),
        name="tail",
    )(*args)


def merger_kernel(*refs):
    blocks, tokens, outs, weight = refs[:4], refs[4:8], refs[8:12], refs[12]
    for hop in range(4):
        for zh in range(4):
            for k in range(5):
                start = zh * 160 + hop * 40 + k * 8
                weight[start : start + 8, :] = blocks[hop][zh, :, 512 * k : 512 * k + 512]
    for hop in range(4):
        for c in range(2):
            total = jnp.zeros((64, 512), F32)
            for zh in range(4):
                rows = tokens[hop][c, zh * 64 : zh * 64 + 64, :160]
                total = total + dot(rows, weight[zh * 160 : zh * 160 + 160, :])
            outs[hop][c] = total[:, :D_LM].astype(outs[hop].dtype)


def merger(blocks, tokens):
    return pl.pallas_call(
        merger_kernel,
        out_shape=[jax.ShapeDtypeStruct((2, 64, D_LM), F32 if hop == 0 else BF) for hop in range(4)],
        in_specs=[VMEM] * 8,
        out_specs=[VMEM] * 4,
        scratch_shapes=[pltpu.VMEM((640, 512), BF)],
        cost_estimate=pl.CostEstimate(
            flops=340_000_000, bytes_accessed=3_000_000, transcendentals=0
        ),
        name="merger",
    )(*blocks, *tokens)


def on_device(
    filterbank,
    conv_weight,
    mlp_gain,
    up_weight,
    down_weight,
    post_gain,
    audio_weight,
    patches,
    vision_gain,
    vision_weight,
    retention,
    kept_count,
):
    packed = pack(kept_count, up_weight, down_weight.T, vision_weight)
    packed, filterbank = lax.optimization_barrier((packed, filterbank))
    blocks = lax.all_to_all(packed, "zh", 0, 0)

    span = arrival_spans()
    main = (10 * span[:, None] + jnp.arange(8, dtype=jnp.int32)[None, :]).reshape(-1)
    rest = (10 * span[None, :] + 8 + jnp.arange(2, dtype=jnp.int32)[:, None]).reshape(-1)
    order = jnp.concatenate([main, rest])
    feature = lax.broadcasted_iota(jnp.int32, (D_ENC, D_ENC), 0)
    pick = (feature == order[None, :]).astype(BF)
    conv = dot(conv_weight, pick).astype(BF)
    audio_rows = lax.dot_general(
        pick, audio_weight, (((0,), (0,)), ((), ())), preferred_element_type=F32
    ).astype(BF)
    gains = jnp.dot(
        jnp.stack([mlp_gain, post_gain]), pick.astype(F32), precision=lax.Precision.HIGHEST
    )

    framed = halo(filterbank)
    unfolded = jnp.concatenate([framed[:-2], framed[1:-1], framed[2:]], axis=1)
    stem = jax.nn.gelu(dot(unfolded, conv), approximate=False).astype(BF)
    residual = stem.astype(F32)
    hidden = layer_norm(residual, gains[0]).astype(BF)
    pooled_stem = residual.reshape(64, 2, D_ENC).mean(axis=1)

    zl, y, c = lax.axis_index("zl"), lax.axis_index("y"), lax.axis_index("c")
    lane = jnp.arange(2048, dtype=jnp.int32)
    owner, inner = lane // 256, lane % 256
    shift = lambda k: jnp.where(k == 2, 3, jnp.where(k == 3, 2, k))
    owner_y = (y + NY - shift(owner % NY)) % NY
    owner_c = jnp.where(owner < NY, c, 1 - c)
    from_zl = (zl + 4 - shift(inner // 40)) % 4
    column = 40 * (8 * from_zl + 2 * owner_y + owner_c) + inner % 40
    column = jnp.where(inner < 160, column, -1)
    patch_feature = lax.broadcasted_iota(jnp.int32, (D_ENC, 2048), 0)
    pick_patch = (patch_feature == column[None, :]).astype(BF)
    patch_normed = rms_norm(patches.astype(F32), vision_gain).astype(BF)
    by_quarter = patch_normed.reshape(64, 4, D_ENC).transpose(1, 0, 2).reshape(256, D_ENC)
    slices = dot(by_quarter, pick_patch).astype(BF)
    core_slices = swap_core(slices[:, 1024:])
    ranks = jnp.arange(MRG_FRAME, dtype=jnp.int32)
    by_rank = (retention[0][:, None] == ranks[None, :]).astype(BF)

    blocks, hidden, pooled_stem, slices, core_slices = lax.optimization_barrier(
        (blocks, hidden, pooled_stem, slices, core_slices)
    )
    ffn_z = jnp.concatenate(around(blocks[:, :, :WIDE], Z, NZ), axis=1)
    tokens = []
    for hop, step in enumerate((0, 1, 3, 2)):
        lanes = slice(256 * hop, 256 * hop + 256)
        pair = jnp.stack([slices[:, lanes], core_slices[:, lanes]])
        back = [(i, (i - step) % NY) for i in range(NY)]
        tokens.append(pair if hop == 0 else lax.ppermute(pair, "y", back))
    ffn_z, tokens = lax.optimization_barrier((ffn_z, tokens))
    spread = jnp.broadcast_to(ffn_z[None], (NY,) + ffn_z.shape)
    own = lax.all_to_all(spread, "y", 0, 0).reshape(512, WIDE)
    vis_blocks = around(blocks[:, :, WIDE:], Z, NZ)
    partials = merger(vis_blocks, tokens)
    summed = partials[0]
    for hop, step in enumerate((1, 3, 2)):
        home = [(i, (i + step) % NY) for i in range(NY)]
        summed = summed + lax.ppermute(partials[1 + hop], "y", home).astype(F32)
    own, summed, audio_rows, by_rank, post = lax.optimization_barrier(
        (own, summed, audio_rows, by_rank, gains[1:])
    )
    theirs = swap_core(summed[1].astype(BF))

    parts, counts = ffn(hidden, own, swap_core(own))
    parts = lax.all_to_all(parts, "mod", 0, 0)
    placed = counts[:, 0].astype(jnp.int32) + AUD_TOK

    me = lax.axis_index(TM).astype(jnp.int32)
    ids = jnp.arange(N_TM, dtype=jnp.int32)
    source = 8 * (ids % NZ) + ids // NZ
    began = jnp.sum(jnp.where(span[None, :] < source[:, None], placed[None, :], 0), axis=1)
    length = jnp.sum(jnp.where(span[None, :] == source[:, None], placed[None, :], 0), axis=1)
    first_slot = jnp.sum(jnp.where(span < me, placed, 0))
    kept = kept_count[0]

    local = ((ids - first_slot) % N_TM)[:, None]
    both = jnp.concatenate([ranks, ranks + kept])
    live = jnp.concatenate([ranks < kept, ranks >= 0])
    take = ((local == both[None, :]) & live[None, :]).astype(BF)
    send = tail(parts, pooled_stem, post, audio_rows, summed[0], theirs, by_rank, take)
    moved = lax.all_to_all(send.reshape(NZ, NY * NC, D_LM), Z, 0, 0)
    moved = lax.all_to_all(moved.transpose(1, 0, 2), ("y", "c"), 0, 0)
    moved = moved.reshape(N_TM, D_LM)

    offset = (me - began) % N_TM
    slot = jnp.where(offset < length, (began + offset) // N_TM, -1)
    slots = jnp.arange(SEQ_DEV, dtype=jnp.int32)
    put = (slot[None, :] == slots[:, None]).astype(BF)
    return dot(put, moved).astype(BF)[None]


def solution(mesh):
    split = Mesh(mesh.devices.reshape(4, 4, NY, NC, NM), TM + ("mod",))
    return jax.shard_map(
        on_device,
        mesh=split,
        in_specs=(
            P(TM, None),
            P(),
            P(),
            P(TM, "mod"),
            P("mod", TM),
            P(),
            P(None, "mod"),
            P(TM, None),
            P(),
            P(TM, "mod"),
            P(TM, None),
            P(TM),
        ),
        out_specs=P(TM, None, "mod"),
        check_vma=False,
    )
```

```python
import jax
import jax.numpy as jnp
from jax import lax
from jax.experimental import pallas as pl
from jax.experimental.pallas import tpu as pltpu
from jax.sharding import Mesh, PartitionSpec as P


MRG_FRAME = 64
AUD_TOK = 64
SEQ_DEV = 96
D_ENC = 1280
D_LM = 448
Z = ("zh", "zl")
TM = Z + ("y", "c")
NZ, NY, NC, NM = 16, 4, 2, 4
WIDE = 3328
N_TM = NZ * NY * NC

BF = jnp.bfloat16
F32 = jnp.float32
NT = (((1,), (1,)), ((), ()))
VMEM = pl.BlockSpec(memory_space=pltpu.VMEM)


def arrival_spans():
    zl, c = lax.axis_index("zl"), lax.axis_index("c")
    block = jnp.arange(N_TM, dtype=jnp.int32)
    hop, zh, z_hop = block // NZ, (block // 4) % 4, block % 4
    shift = lambda k: jnp.where(k == 2, 3, jnp.where(k == 3, 2, k))
    from_z = 4 * zh + (zl + 4 - shift(z_hop)) % 4
    from_y = hop % NY
    from_c = jnp.where(hop < NY, c, 1 - c)
    return (8 * from_z + 2 * from_y + from_c).astype(jnp.int32)


def around(value, axis, size):
    shifts = (1, size - 1, 2)
    return [value] + [
        lax.ppermute(value, axis, [(i, (i + shift) % size) for i in range(size)])
        for shift in shifts
    ]


def swap_core(value):
    return lax.ppermute(value, "c", [(0, 1), (1, 0)])


def layer_norm(values, scale_gain):
    average = jnp.mean(values, axis=-1, keepdims=True)
    centred = values - average
    variance = jnp.mean(centred * centred, axis=-1, keepdims=True)
    return centred * lax.rsqrt(variance + 1e-05) * scale_gain


def rms_norm(values, scale_gain):
    square_mean = jnp.mean(values * values, axis=-1, keepdims=True)
    return values * lax.rsqrt(square_mean + 1e-06) * scale_gain


def dot(a, b):
    return jnp.dot(a, b, preferred_element_type=F32)


def erf_gelu(x):
    return 0.5 * x * (1.0 + lax.erf(x * 0.7071067811865476))


def pack_kernel(count_ref, up_ref, down_ref, vision_ref, out_ref):
    sides = (up_ref[8:].astype(F32), down_ref[8:].astype(F32))
    rest = [
        sides[row // 2][row % 2 : row % 2 + 1, 640 * half : 640 * half + 640]
        for half in range(2)
        for row in range(4)
    ]
    rest = jnp.concatenate(rest, axis=0).astype(BF)
    count = jnp.full((8, 128), count_ref[0].astype(F32), F32).astype(BF)
    blank = jnp.zeros((8, 64), BF)
    for peer in range(4):
        out_ref[peer, :, :1280] = up_ref[:8, :]
        out_ref[peer, :, 1280:2560] = down_ref[:8, :]
        out_ref[peer, :, 2560:3200] = rest
        out_ref[peer, :, 3200:WIDE] = count
        for k in range(5):
            start = WIDE + 512 * k
            rows = vision_ref[8 * k : 8 * k + 8, :]
            out_ref[peer, :, start : start + 512] = jnp.concatenate([rows, blank], axis=1)


def pack(kept_count, up_weight, down_rows, vision_weight):
    return pl.pallas_call(
        pack_kernel,
        out_shape=jax.ShapeDtypeStruct((4, 8, WIDE + 2560), BF),
        in_specs=[pl.BlockSpec(memory_space=pltpu.SMEM), VMEM, VMEM, VMEM],
        out_specs=VMEM,
        name="pack",
    )(kept_count, up_weight, down_rows, vision_weight)


def stem_kernel(
    frames_ref, before_ref, after_ref, conv_ref, gain_ref, order_ref, hidden_ref, pooled_ref, post_ref, rows
):
    frames = frames_ref[...].astype(F32)
    earlier = jnp.concatenate([before_ref[...].astype(F32), frames[:-1]], axis=0)
    later = jnp.concatenate([frames[1:], after_ref[...].astype(F32)], axis=0)
    unfolded = jnp.concatenate([earlier.astype(BF), frames_ref[...], later.astype(BF)], axis=1)
    gain = gain_ref[...]
    high = gain.astype(BF)
    middle = (gain - high.astype(F32)).astype(BF)
    low = (gain - high.astype(F32) - middle.astype(F32)).astype(BF)
    rows[:384, :] = conv_ref[...]
    rows[384:392, :] = high
    rows[392:400, :] = middle
    rows[400:408, :] = low
    rows[408:416, :] = jnp.zeros((8, D_ENC), BF)
    moved = jnp.zeros((416, D_ENC), F32)
    order = order_ref[...]
    for k in range(5):
        natural = lax.broadcasted_iota(jnp.int32, (256, D_ENC), 0) + 256 * k
        pick = jnp.where(natural == order, 1.0, 0.0).astype(BF)
        moved = moved + dot(rows[:, 256 * k : 256 * k + 256], pick)
    gains = moved[384:392] + moved[392:400] + moved[400:408]
    stem = erf_gelu(dot(unfolded, moved[:384].astype(BF))).astype(BF)
    hidden_ref[...] = layer_norm(stem.astype(F32), gains[0:1]).astype(BF)
    row = lax.broadcasted_iota(jnp.int32, (64, 128), 0)
    col = lax.broadcasted_iota(jnp.int32, (64, 128), 1)
    pair = jnp.where(col // 2 == row, 0.5, 0.0).astype(BF)
    pooled_ref[...] = dot(pair, stem)
    post_ref[...] = gains[1:2]


def make_stem(*args):
    return pl.pallas_call(
        stem_kernel,
        out_shape=(
            jax.ShapeDtypeStruct((128, D_ENC), BF),
            jax.ShapeDtypeStruct((64, D_ENC), F32),
            jax.ShapeDtypeStruct((1, D_ENC), F32),
        ),
        in_specs=[VMEM] * 6,
        out_specs=(VMEM,) * 3,
        scratch_shapes=[pltpu.VMEM((416, D_ENC), BF)],
        cost_estimate=pl.CostEstimate(
            flops=1_500_000_000, bytes_accessed=2_500_000, transcendentals=170_000
        ),
        name="stem",
    )(*args)


def ffn_kernel(hidden_ref, own_ref, other_ref, out_ref, count_ref, up, down, flat):
    for c, ref in enumerate((own_ref, other_ref)):
        rows = slice(512 * c, 512 * c + 512)
        up[rows, :] = ref[:, :1280]
        down[rows, :] = ref[:, 1280:2560]
        for tile in range(6):
            lanes = slice(2560 + 128 * tile, 2688 + 128 * tile)
            flat[tile, rows, :] = ref[:, lanes].astype(F32)
    for tile in range(5):
        for half in range(2):
            lanes = slice(640 * half + 128 * tile, 640 * half + 128 * tile + 128)
            for row in range(4):
                plane = flat[tile, pl.ds(half * 4 + row, N_TM, stride=8), :].astype(BF)
                into = up if row < 2 else down
                start = 1024 + (row % 2) * N_TM
                into[start : start + N_TM, lanes] = plane
    count_ref[...] = flat[5, pl.ds(0, N_TM, stride=8), :]
    row = lax.broadcasted_iota(jnp.int32, (64, 128), 0)
    col = lax.broadcasted_iota(jnp.int32, (64, 128), 1)
    pair = jnp.where(col // 2 == row, 0.5, 0.0).astype(BF)
    act = erf_gelu(dot(hidden_ref[...], up[...])).astype(BF)
    pooled = dot(pair, act).astype(BF)
    part = lax.dot_general(pooled, down[...], NT, preferred_element_type=F32).astype(BF)
    for peer in range(NM):
        out_ref[peer] = part


def ffn(hidden, own, other):
    return pl.pallas_call(
        ffn_kernel,
        out_shape=(
            jax.ShapeDtypeStruct((NM, 64, D_ENC), BF),
            jax.ShapeDtypeStruct((N_TM, 128), F32),
        ),
        in_specs=[VMEM] * 3,
        out_specs=(VMEM, VMEM),
        scratch_shapes=[
            pltpu.VMEM((1280, 1280), BF),
            pltpu.VMEM((1280, 1280), BF),
            pltpu.VMEM((6, 1024, 128), F32),
        ],
        cost_estimate=pl.CostEstimate(
            flops=650_000_000, bytes_accessed=8_000_000, transcendentals=170_000
        ),
        name="ffn",
    )(hidden, own, other)


def tail_kernel(
    place_ref, part_ref, stem_ref, gain_ref, audio_ref, vis_ref, rank_ref, count_ref, span_ref, out_ref
):
    me, kept = place_ref[0], place_ref[1]
    placed = count_ref[...] + float(AUD_TOK)
    slot = jnp.sum(jnp.where(span_ref[...] < me, placed, 0.0), axis=0, keepdims=True)
    row = lax.broadcasted_iota(jnp.int32, (N_TM, 128), 0)
    col = lax.broadcasted_iota(jnp.int32, (N_TM, 128), 1)
    local = (row - slot.astype(jnp.int32)) & (N_TM - 1)
    rank = jnp.where(col < 64, col, col - 64 + kept)
    take = (local == rank) & ((col >= 64) | (col < kept))
    take = jnp.where(take, 1.0, 0.0).astype(BF)
    total = stem_ref[...]
    for peer in range(NM):
        total = total + part_ref[peer].astype(F32)
    normed = layer_norm(total, gain_ref[...]).astype(BF)
    audio = dot(normed, audio_ref[...]).astype(BF)
    visual = vis_ref[0].astype(F32)
    for peer in range(1, 8):
        visual = visual + vis_ref[peer].astype(F32)
    visual = dot(rank_ref[...], visual.astype(BF)).astype(BF)
    picked = dot(take[:, :64], visual) + dot(take[:, 64:], audio)
    out_ref[...] = picked.astype(BF)


def tail(*args):
    return pl.pallas_call(
        tail_kernel,
        out_shape=jax.ShapeDtypeStruct((N_TM, D_LM), BF),
        in_specs=[pl.BlockSpec(memory_space=pltpu.SMEM)] + [VMEM] * 8,
        out_specs=VMEM,
        cost_estimate=pl.CostEstimate(
            flops=80_000_000, bytes_accessed=2_500_000, transcendentals=64
        ),
        name="tail",
    )(*args)


def merger_kernel(place_ref, *refs):
    blocks, tokens, out_ref, weight = refs[:4], refs[4:8], refs[8], refs[9]
    for hop in range(4):
        for zh in range(4):
            for k in range(5):
                start = zh * 160 + hop * 40 + k * 8
                weight[start : start + 8, :] = blocks[hop][zh, :, 512 * k : 512 * k + 512]
    for hop in range(4):
        for c in range(2):
            total = jnp.zeros((64, 512), F32)
            for zh in range(4):
                rows = tokens[hop][c, zh * 64 : zh * 64 + 64, :160]
                total = total + dot(rows, weight[zh * 160 : zh * 160 + 160, :])
            out_ref[place_ref[2 * hop + c]] = total[:, :D_LM].astype(BF)


def merger(place, blocks, tokens):
    return pl.pallas_call(
        merger_kernel,
        out_shape=jax.ShapeDtypeStruct((8, 64, D_LM), BF),
        in_specs=[pl.BlockSpec(memory_space=pltpu.SMEM)] + [VMEM] * 8,
        out_specs=VMEM,
        scratch_shapes=[pltpu.VMEM((640, 512), BF)],
        cost_estimate=pl.CostEstimate(
            flops=340_000_000, bytes_accessed=3_000_000, transcendentals=0
        ),
        name="merger",
    )(place, *blocks, *tokens)


def on_device(
    filterbank,
    conv_weight,
    mlp_gain,
    up_weight,
    down_weight,
    post_gain,
    audio_weight,
    patches,
    vision_gain,
    vision_weight,
    retention,
    kept_count,
):
    packed = pack(kept_count, up_weight, down_weight.T, vision_weight)
    packed, filterbank = lax.optimization_barrier((packed, filterbank))
    blocks = lax.all_to_all(packed, "zh", 0, 0)

    span = arrival_spans()
    main = (10 * span[:, None] + jnp.arange(8, dtype=jnp.int32)[None, :]).reshape(-1)
    rest = (10 * span[None, :] + 8 + jnp.arange(2, dtype=jnp.int32)[:, None]).reshape(-1)
    order = jnp.concatenate([main, rest])
    feature = lax.broadcasted_iota(jnp.int32, (D_ENC, D_ENC), 0)
    pick = (feature == order[None, :]).astype(BF)
    audio_rows = lax.dot_general(
        pick, audio_weight, (((0,), (0,)), ((), ())), preferred_element_type=F32
    ).astype(BF)
    up = [(i, i + 1) for i in range(N_TM - 1)]
    before = lax.ppermute(filterbank[-1:], TM, up)
    after = lax.ppermute(filterbank[:1], TM, [(j, i) for i, j in up])
    both_gains = jnp.pad(jnp.stack([mlp_gain, post_gain]), ((0, 6), (0, 0)))

    zl, y, c = lax.axis_index("zl"), lax.axis_index("y"), lax.axis_index("c")
    lane = jnp.arange(2048, dtype=jnp.int32)
    owner, inner = lane // 256, lane % 256
    shift = lambda k: jnp.where(k == 2, 3, jnp.where(k == 3, 2, k))
    owner_y = (y + NY - shift(owner % NY)) % NY
    owner_c = jnp.where(owner < NY, c, 1 - c)
    from_zl = (zl + 4 - shift(inner // 40)) % 4
    column = 40 * (8 * from_zl + 2 * owner_y + owner_c) + inner % 40
    column = jnp.where(inner < 160, column, -1)
    patch_feature = lax.broadcasted_iota(jnp.int32, (D_ENC, 2048), 0)
    pick_patch = (patch_feature == column[None, :]).astype(BF)
    patch_normed = rms_norm(patches.astype(F32), vision_gain).astype(BF)
    by_quarter = patch_normed.reshape(64, 4, D_ENC).transpose(1, 0, 2).reshape(256, D_ENC)
    slices = dot(by_quarter, pick_patch).astype(BF)
    core_slices = swap_core(slices[:, 1024:])
    ranks = jnp.arange(MRG_FRAME, dtype=jnp.int32)
    by_rank = (retention[0][:, None] == ranks[None, :]).astype(BF)

    ffn_hops = around(blocks[:, :, :WIDE], Z, NZ)
    tokens = []
    for hop, step in enumerate((0, 1, 3, 2)):
        lanes = slice(256 * hop, 256 * hop + 256)
        pair = jnp.stack([slices[:, lanes], core_slices[:, lanes]])
        back = [(i, (i - step) % NY) for i in range(NY)]
        tokens.append(pair if hop == 0 else lax.ppermute(pair, "y", back))
    ffn_z = jnp.concatenate(ffn_hops, axis=1)
    spread = jnp.broadcast_to(ffn_z[None], (NY,) + ffn_z.shape)
    own = lax.all_to_all(spread, "y", 0, 0).reshape(512, WIDE)
    hidden, pooled_stem, post = make_stem(
        filterbank, before, after, conv_weight, both_gains, order[None, :]
    )
    steps = jnp.asarray([0, 0, 1, 1, 3, 3, 2, 2], jnp.int32)
    flips = jnp.asarray([0, 1] * 4, jnp.int32)
    place = 2 * ((y + steps) % NY) + jnp.where(flips == 1, 1 - c, c)
    vis_hops = around(blocks[:, :, WIDE:], Z, NZ)
    partials = merger(place.astype(jnp.int32), vis_hops, tokens)
    partials = lax.all_to_all(partials, ("y", "c"), 0, 0)
    own, audio_rows, by_rank, hidden = lax.optimization_barrier(
        (own, audio_rows, by_rank, hidden)
    )
    other = swap_core(own)
    parts, counts = ffn(hidden, own, other)
    parts = lax.all_to_all(parts, "mod", 0, 0)
    me = lax.axis_index(TM).astype(jnp.int32)
    ids = jnp.arange(N_TM, dtype=jnp.int32)
    wide_span = jnp.broadcast_to(span[:, None], (N_TM, 128))
    ours = jnp.stack([me, kept_count[0]])
    send = tail(
        ours, parts, pooled_stem, post, audio_rows, partials, by_rank, counts, wide_span
    )
    counts, send = lax.optimization_barrier((counts, send))
    placed = counts[:, 0].astype(jnp.int32) + AUD_TOK
    began = jnp.sum(jnp.where(span[None, :] < ids[:, None], placed[None, :], 0), axis=1)
    length = jnp.sum(jnp.where(span[None, :] == ids[:, None], placed[None, :], 0), axis=1)
    moved = lax.all_to_all(send.reshape(N_TM, 1, D_LM), TM, 0, 0).reshape(N_TM, D_LM)

    offset = (me - began) % N_TM
    slot = jnp.where(offset < length, (began + offset) // N_TM, -1)
    slots = jnp.arange(SEQ_DEV, dtype=jnp.int32)
    put = (slot[None, :] == slots[:, None]).astype(BF)
    return dot(put, moved).astype(BF)[None]


def solution(mesh):
    split = Mesh(mesh.devices.reshape(4, 4, NY, NC, NM), TM + ("mod",))
    return jax.shard_map(
        on_device,
        mesh=split,
        in_specs=(
            P(TM, None),
            P(),
            P(),
            P(TM, "mod"),
            P("mod", TM),
            P(),
            P(None, "mod"),
            P(TM, None),
            P(),
            P(TM, "mod"),
            P(TM, None),
            P(TM),
        ),
        out_specs=P(TM, None, "mod"),
        check_vma=False,
    )
```

```python
import jax
import jax.numpy as jnp
from jax import lax
from jax.experimental import pallas as pl
from jax.experimental.pallas import tpu as pltpu
from jax.sharding import Mesh, PartitionSpec as P


AUD_TOK = 64
SEQ_DEV = 96
D_ENC = 1280
D_LM = 448
Z = ("zh", "zl")
TM = Z + ("y", "c")
NZ, NY, NC, NM = 16, 4, 2, 4
WIDE = 3328
N_TM = NZ * NY * NC

BF = jnp.bfloat16
F32 = jnp.float32
NT = (((1,), (1,)), ((), ()))
TN = (((0,), (0,)), ((), ()))
VMEM = pl.BlockSpec(memory_space=pltpu.VMEM)


def arrival_spans():
    zl, c = lax.axis_index("zl"), lax.axis_index("c")
    block = jnp.arange(N_TM, dtype=jnp.int32)
    hop, zh, z_hop = block // NZ, (block // 4) % 4, block % 4
    shift = lambda k: jnp.where(k == 2, 3, jnp.where(k == 3, 2, k))
    from_z = 4 * zh + (zl + 4 - shift(z_hop)) % 4
    from_y = hop % NY
    from_c = jnp.where(hop < NY, c, 1 - c)
    return (8 * from_z + 2 * from_y + from_c).astype(jnp.int32)


def around(value, axis, size):
    shifts = (1, size - 1, 2)
    return [value] + [
        lax.ppermute(value, axis, [(i, (i + shift) % size) for i in range(size)])
        for shift in shifts
    ]


def swap_core(value):
    return lax.ppermute(value, "c", [(0, 1), (1, 0)])


def layer_norm(values, scale_gain):
    average = jnp.mean(values, axis=-1, keepdims=True)
    centred = values - average
    variance = jnp.mean(centred * centred, axis=-1, keepdims=True)
    return centred * lax.rsqrt(variance + 1e-05) * scale_gain


def rms_norm(values, scale_gain):
    square_mean = jnp.mean(values * values, axis=-1, keepdims=True)
    return values * lax.rsqrt(square_mean + 1e-06) * scale_gain


def dot(a, b):
    return jnp.dot(a, b, preferred_element_type=F32)


def erf_gelu(x):
    return 0.5 * x * (1.0 + lax.erf(x * 0.7071067811865476))


def pack_kernel(count_ref, up_ref, down_ref, vision_ref, out_ref):
    sides = (up_ref[8:].astype(F32), down_ref[8:].astype(F32))
    rest = [
        sides[row // 2][row % 2 : row % 2 + 1, 640 * half : 640 * half + 640]
        for half in range(2)
        for row in range(4)
    ]
    rest = jnp.concatenate(rest, axis=0).astype(BF)
    count = jnp.full((8, 128), count_ref[0].astype(F32), F32).astype(BF)
    blank = jnp.zeros((8, 64), BF)
    for peer in range(4):
        out_ref[peer, :, :1280] = up_ref[:8, :]
        out_ref[peer, :, 1280:2560] = down_ref[:8, :]
        out_ref[peer, :, 2560:3200] = rest
        out_ref[peer, :, 3200:WIDE] = count
        for k in range(5):
            start = WIDE + 512 * k
            rows = vision_ref[8 * k : 8 * k + 8, :]
            out_ref[peer, :, start : start + 512] = jnp.concatenate([rows, blank], axis=1)


def pack(kept_count, up_weight, down_rows, vision_weight):
    return pl.pallas_call(
        pack_kernel,
        out_shape=jax.ShapeDtypeStruct((4, 8, WIDE + 2560), BF),
        in_specs=[pl.BlockSpec(memory_space=pltpu.SMEM), VMEM, VMEM, VMEM],
        out_specs=VMEM,
        name="pack",
    )(kept_count, up_weight, down_rows, vision_weight)


def stem_kernel(
    frames_ref, before_ref, after_ref, conv_ref, gain_ref, order_ref, hidden_ref, pooled_ref, post_ref, rows
):
    frames = frames_ref[...].astype(F32)
    earlier = jnp.concatenate([before_ref[...].astype(F32), frames[:-1]], axis=0)
    later = jnp.concatenate([frames[1:], after_ref[...].astype(F32)], axis=0)
    unfolded = jnp.concatenate([earlier.astype(BF), frames_ref[...], later.astype(BF)], axis=1)
    gain = gain_ref[...]
    high = gain.astype(BF)
    middle = (gain - high.astype(F32)).astype(BF)
    low = (gain - high.astype(F32) - middle.astype(F32)).astype(BF)
    rows[:384, :] = conv_ref[...]
    rows[384:392, :] = high
    rows[392:400, :] = middle
    rows[400:408, :] = low
    rows[408:416, :] = jnp.zeros((8, D_ENC), BF)
    moved = jnp.zeros((416, D_ENC), F32)
    order = order_ref[...]
    for k in range(5):
        natural = lax.broadcasted_iota(jnp.int32, (256, D_ENC), 0) + 256 * k
        pick = jnp.where(natural == order, 1.0, 0.0).astype(BF)
        moved = moved + dot(rows[:, 256 * k : 256 * k + 256], pick)
    gains = moved[384:392] + moved[392:400] + moved[400:408]
    stem = erf_gelu(dot(unfolded, moved[:384].astype(BF))).astype(BF)
    hidden_ref[...] = layer_norm(stem.astype(F32), gains[0:1]).astype(BF)
    row = lax.broadcasted_iota(jnp.int32, (64, 128), 0)
    col = lax.broadcasted_iota(jnp.int32, (64, 128), 1)
    pair = jnp.where(col // 2 == row, 0.5, 0.0).astype(BF)
    pooled_ref[...] = dot(pair, stem)
    post_ref[...] = gains[1:2]


def make_stem(*args):
    return pl.pallas_call(
        stem_kernel,
        out_shape=(
            jax.ShapeDtypeStruct((128, D_ENC), BF),
            jax.ShapeDtypeStruct((64, D_ENC), F32),
            jax.ShapeDtypeStruct((1, D_ENC), F32),
        ),
        in_specs=[VMEM] * 6,
        out_specs=(VMEM,) * 3,
        scratch_shapes=[pltpu.VMEM((416, D_ENC), BF)],
        cost_estimate=pl.CostEstimate(
            flops=1_500_000_000, bytes_accessed=2_500_000, transcendentals=170_000
        ),
        compiler_params=pltpu.CompilerParams(vmem_limit_bytes=16 << 20),
        name="stem",
    )(*args)


def ffn_kernel(hidden_ref, own_ref, other_ref, out_ref, count_ref, up, down, flat):
    for c, ref in enumerate((own_ref, other_ref)):
        rows = slice(512 * c, 512 * c + 512)
        up[rows, :] = ref[:, :1280]
        down[rows, :] = ref[:, 1280:2560]
        for tile in range(6):
            lanes = slice(2560 + 128 * tile, 2688 + 128 * tile)
            flat[tile, rows, :] = ref[:, lanes].astype(F32)
    for tile in range(5):
        for half in range(2):
            lanes = slice(640 * half + 128 * tile, 640 * half + 128 * tile + 128)
            for row in range(4):
                plane = flat[tile, pl.ds(half * 4 + row, N_TM, stride=8), :].astype(BF)
                into = up if row < 2 else down
                start = 1024 + (row % 2) * N_TM
                into[start : start + N_TM, lanes] = plane
    count_ref[...] = flat[5, pl.ds(0, N_TM, stride=8), :]
    row = lax.broadcasted_iota(jnp.int32, (64, 128), 0)
    col = lax.broadcasted_iota(jnp.int32, (64, 128), 1)
    pair = jnp.where(col // 2 == row, 0.5, 0.0).astype(BF)
    act = erf_gelu(dot(hidden_ref[...], up[...])).astype(BF)
    pooled = dot(pair, act).astype(BF)
    part = lax.dot_general(pooled, down[...], NT, preferred_element_type=F32).astype(BF)
    for peer in range(NM):
        out_ref[peer] = part


def ffn(hidden, own, other):
    return pl.pallas_call(
        ffn_kernel,
        out_shape=(
            jax.ShapeDtypeStruct((NM, 64, D_ENC), BF),
            jax.ShapeDtypeStruct((N_TM, 128), F32),
        ),
        in_specs=[VMEM] * 3,
        out_specs=(VMEM, VMEM),
        scratch_shapes=[
            pltpu.VMEM((1280, 1280), BF),
            pltpu.VMEM((1280, 1280), BF),
            pltpu.VMEM((6, 1024, 128), F32),
        ],
        cost_estimate=pl.CostEstimate(
            flops=650_000_000, bytes_accessed=8_000_000, transcendentals=170_000
        ),
        compiler_params=pltpu.CompilerParams(vmem_limit_bytes=32 << 20),
        name="ffn",
    )(hidden, own, other)


def tail_kernel(
    place_ref, part_ref, stem_ref, gain_ref, audio_ref, vis_ref, rank_ref, count_ref, span_ref, out_ref
):
    me, kept = place_ref[0], place_ref[1]
    placed = count_ref[...] + float(AUD_TOK)
    slot = jnp.sum(jnp.where(span_ref[...] < me, placed, 0.0), axis=0, keepdims=True)
    row = lax.broadcasted_iota(jnp.int32, (N_TM, 128), 0)
    col = lax.broadcasted_iota(jnp.int32, (N_TM, 128), 1)
    local = (row - slot.astype(jnp.int32)) & (N_TM - 1)
    rank = jnp.where(col < 64, col, col - 64 + kept)
    take = (local == rank) & ((col >= 64) | (col < kept))
    take = jnp.where(take, 1.0, 0.0).astype(BF)
    total = stem_ref[...]
    for peer in range(NM):
        total = total + part_ref[peer].astype(F32)
    normed = layer_norm(total, gain_ref[...]).astype(BF)
    audio = dot(normed, audio_ref[...]).astype(BF)
    visual = vis_ref[0].astype(F32)
    for peer in range(1, 8):
        visual = visual + vis_ref[peer].astype(F32)
    token = lax.broadcasted_iota(jnp.int32, (64, 64), 0)
    by_rank = jnp.where(token == rank_ref[...], 1.0, 0.0).astype(BF)
    visual = lax.dot_general(by_rank, visual.astype(BF), TN, preferred_element_type=F32).astype(BF)
    picked = dot(take[:, :64], visual) + dot(take[:, 64:], audio)
    out_ref[...] = picked.astype(BF)


def tail(*args):
    return pl.pallas_call(
        tail_kernel,
        out_shape=jax.ShapeDtypeStruct((N_TM, D_LM), BF),
        in_specs=[pl.BlockSpec(memory_space=pltpu.SMEM)] + [VMEM] * 8,
        out_specs=VMEM,
        cost_estimate=pl.CostEstimate(
            flops=80_000_000, bytes_accessed=2_500_000, transcendentals=64
        ),
        compiler_params=pltpu.CompilerParams(vmem_limit_bytes=12 << 20),
        name="tail",
    )(*args)


def merger_kernel(place_ref, *refs):
    blocks, nearby, tokens, out_ref, weight = refs[:4], refs[4:6], refs[6:9], refs[9], refs[10]
    for hop in range(4):
        for zh in range(4):
            for k in range(5):
                start = zh * 160 + hop * 40 + k * 8
                weight[start : start + 8, :] = blocks[hop][zh, :, 512 * k : 512 * k + 512]
    for hop in range(4):
        for c in range(2):
            total = jnp.zeros((64, 512), F32)
            for zh in range(4):
                span = slice(zh * 64, zh * 64 + 64)
                rows = nearby[c][span, :160] if hop == 0 else tokens[hop - 1][c, span, :160]
                total = total + dot(rows, weight[zh * 160 : zh * 160 + 160, :])
            out_ref[place_ref[2 * hop + c]] = total[:, :D_LM].astype(BF)


def merger(place, blocks, nearby, tokens):
    return pl.pallas_call(
        merger_kernel,
        out_shape=jax.ShapeDtypeStruct((8, 64, D_LM), BF),
        in_specs=[pl.BlockSpec(memory_space=pltpu.SMEM)] + [VMEM] * 9,
        out_specs=VMEM,
        scratch_shapes=[pltpu.VMEM((640, 512), BF)],
        cost_estimate=pl.CostEstimate(
            flops=340_000_000, bytes_accessed=3_000_000, transcendentals=0
        ),
        compiler_params=pltpu.CompilerParams(vmem_limit_bytes=12 << 20),
        name="merger",
    )(place, *blocks, *nearby, *tokens)


def on_device(
    filterbank,
    conv_weight,
    mlp_gain,
    up_weight,
    down_weight,
    post_gain,
    audio_weight,
    patches,
    vision_gain,
    vision_weight,
    retention,
    kept_count,
):
    packed = pack(kept_count, up_weight, down_weight.T, vision_weight)
    packed, filterbank, patches = lax.optimization_barrier((packed, filterbank, patches))
    blocks = lax.all_to_all(packed, "zh", 0, 0)

    span = arrival_spans()
    main = (10 * span[:, None] + jnp.arange(8, dtype=jnp.int32)[None, :]).reshape(-1)
    rest = (10 * span[None, :] + 8 + jnp.arange(2, dtype=jnp.int32)[:, None]).reshape(-1)
    order = jnp.concatenate([main, rest])
    up = [(i, i + 1) for i in range(N_TM - 1)]
    before = lax.ppermute(filterbank[-1:], TM, up)
    after = lax.ppermute(filterbank[:1], TM, [(j, i) for i, j in up])
    both_gains = jnp.pad(jnp.stack([mlp_gain, post_gain]), ((0, 6), (0, 0)))

    zl, y, c = lax.axis_index("zl"), lax.axis_index("y"), lax.axis_index("c")
    lane = jnp.arange(2048, dtype=jnp.int32)
    owner, inner = lane // 256, lane % 256
    shift = lambda k: jnp.where(k == 2, 3, jnp.where(k == 3, 2, k))
    owner_y = (y + NY - shift(owner % NY)) % NY
    owner_c = jnp.where(owner < NY, c, 1 - c)
    from_zl = (zl + 4 - shift(inner // 40)) % 4
    column = 40 * (8 * from_zl + 2 * owner_y + owner_c) + inner % 40
    column = jnp.where(inner < 160, column, -1)
    patch_feature = lax.broadcasted_iota(jnp.int32, (D_ENC, 2048), 0)
    pick_patch = (patch_feature == column[None, :]).astype(BF)
    patch_normed = rms_norm(patches.astype(F32), vision_gain).astype(BF)
    by_quarter = patch_normed.reshape(64, 4, D_ENC).transpose(1, 0, 2).reshape(256, D_ENC)
    slices = dot(by_quarter, pick_patch).astype(BF)
    core_slices = swap_core(slices[:, 1024:])
    ffn_hops = around(blocks[:, :, :WIDE], Z, NZ)
    tokens = []
    for hop, step in enumerate((1, 3, 2)):
        lanes = slice(256 * hop + 256, 256 * hop + 512)
        pair = jnp.stack([slices[:, lanes], core_slices[:, lanes]])
        back = [(i, (i - step) % NY) for i in range(NY)]
        tokens.append(lax.ppermute(pair, "y", back))
    steps = jnp.asarray([0, 0, 1, 1, 3, 3, 2, 2], jnp.int32)
    flips = jnp.asarray([0, 1] * 4, jnp.int32)
    place = (2 * ((y + steps) % NY) + jnp.where(flips == 1, 1 - c, c)).astype(jnp.int32)
    ffn_z = jnp.concatenate(ffn_hops, axis=1)
    vis_block, order_row = blocks[:, :, WIDE:], order[None, :]
    nearby = (slices[:, :256], core_slices[:, :256])
    spread = jnp.broadcast_to(ffn_z[None], (NY,) + ffn_z.shape)
    own = lax.all_to_all(spread, "y", 0, 0).reshape(512, WIDE)
    hidden, pooled_stem, post = make_stem(
        filterbank, before, after, conv_weight, both_gains, order_row
    )
    vis_hops = around(vis_block, Z, NZ)
    partials = merger(place, vis_hops, nearby, tokens)
    partials = lax.all_to_all(partials, ("y", "c"), 0, 0)
    own, hidden = lax.optimization_barrier((own, hidden))
    other = swap_core(own)
    parts, counts = ffn(hidden, own, other)
    parts, audio_weight = lax.optimization_barrier((parts, audio_weight))
    feature = lax.broadcasted_iota(jnp.int32, (D_ENC, D_ENC), 0)
    pick = (feature == order[None, :]).astype(BF)
    audio_rows = lax.dot_general(
        pick, audio_weight, (((0,), (0,)), ((), ())), preferred_element_type=F32
    ).astype(BF)
    parts = lax.all_to_all(parts, "mod", 0, 0)
    me = lax.axis_index(TM).astype(jnp.int32)
    ids = jnp.arange(N_TM, dtype=jnp.int32)
    wide_span = jnp.broadcast_to(span[:, None], (N_TM, 128))
    ours = jnp.stack([me, kept_count[0]])
    send = tail(
        ours, parts, pooled_stem, post, audio_rows, partials, retention, counts, wide_span
    )
    counts, send = lax.optimization_barrier((counts, send))
    placed = counts[:, 0].astype(jnp.int32) + AUD_TOK
    began = jnp.sum(jnp.where(span[None, :] < ids[:, None], placed[None, :], 0), axis=1)
    length = jnp.sum(jnp.where(span[None, :] == ids[:, None], placed[None, :], 0), axis=1)
    moved = lax.all_to_all(send.reshape(N_TM, 1, D_LM), TM, 0, 0).reshape(N_TM, D_LM)

    offset = (me - began) % N_TM
    slot = jnp.where(offset < length, (began + offset) // N_TM, -1)
    slots = jnp.arange(SEQ_DEV, dtype=jnp.int32)
    put = (slot[None, :] == slots[:, None]).astype(BF)
    return dot(put, moved).astype(BF)[None]


def solution(mesh):
    split = Mesh(mesh.devices.reshape(4, 4, NY, NC, NM), TM + ("mod",))
    return jax.shard_map(
        on_device,
        mesh=split,
        in_specs=(
            P(TM, None),
            P(),
            P(),
            P(TM, "mod"),
            P("mod", TM),
            P(),
            P(None, "mod"),
            P(TM, None),
            P(),
            P(TM, "mod"),
            P(TM, None),
            P(TM),
        ),
        out_specs=P(TM, None, "mod"),
        check_vma=False,
    )
```
